32 devices in a mesh: dp: 4 (over y, x), seq: 8 (over z, core).
Axes of the slice: x: 2, y: 2, z: 4, core: 2. Of those that a mesh axis runs over, the one named last changes fastest.
Arguments:
- queries: bfloat16 [16, 4096, 128], P(None, ('dp', 'seq')), parts along dimension 1, may hold values from -6 to 6
- key_pairs: bfloat16 [16, 4096, 256], P(None, ('dp', 'seq')), parts along dimension 1, may hold values from -6 to 6
- value_pairs: bfloat16 [16, 4096, 256], P(None, ('dp', 'seq')), parts along dimension 1, may hold values from -6 to 6
- strengths: float32 [16, 8192], P(None, ('dp', 'seq')), parts along dimension 1, may hold values from 0.002 to 1.99
- decays: float32 [16, 4096], P(None, ('dp', 'seq')), parts along dimension 1, may hold values from 0 to 1, as said below
- conv_query: float32 [16, 4, 128], replicated, may hold values from -1.5 to 1.5
- conv_key: float32 [16, 4, 256], replicated, may hold values from -1.5 to 1.5
- conv_value: float32 [16, 4, 256], replicated, may hold values from -1.5 to 1.5
- doc_lengths: int32 [32], P('dp'), parts along dimension 0, may hold values from 1 to 512, 1024 in all
Outputs:
- readout: bfloat16 [16, 4096, 128], P(None, ('dp', 'seq')), parts along dimension 1
The draws below stay inside these ranges and needn't reach their ends.
There are 4 independent parts, one for each index of `dp`. The reference program is written for one: setup_inputs(seed, part) draws one part's arguments, and reference() takes and returns one part's arrays. A program takes and returns all parts, laid end to end along the dimension named above; an argument that names none is the same for every part. Nothing has to cross between parts.
Inputs may be any that keep to these rules, and one draw needn't show every extreme that they name: `doc_lengths`: they sum to 1024, and the longest document has exactly 512 tokens. Every gate exp(-decays) lies between 0.36 and 1.
All inputs are finite; a program needn't handle non-finite values.
Results may differ from the reference program's by a relative error of at most 0.0062.
Values may be sent and summed in bfloat16 or wider, within the bound.
A program may use at most 320 MiB of HBM per device.

```python
import math
import jax
import jax.numpy as jnp
import numpy as np
from jax import lax

HEAD_COUNT = 16
DK = 128
DV = 128
TAPS = 4
LONGEST_DOC = 4
TOKENS_PER_SHARD = 128
PACKED_TOKENS = 1024
MOST = 512
NDOCS = 8
N_SEQ = 8


def head_speed(key):
    picker = jax.random.uniform(jax.random.fold_in(key, 101), (HEAD_COUNT,))
    return picker < 0.5


def draw_decays(key, part):
    fast = head_speed(key)
    parallel_lanes = jax.random.split(jax.random.fold_in(key, 202), 6)
    fast_rate = jnp.exp(jax.random.uniform(parallel_lanes[0], (HEAD_COUNT,), jnp.float32, jnp.log(1.0 / 50.0), jnp.log(1.0 / 30.0)))
    slow_rate = jnp.exp(jax.random.uniform(parallel_lanes[1], (HEAD_COUNT,), jnp.float32, jnp.log(0.05), jnp.log(0.4))) / (LONGEST_DOC * TOKENS_PER_SHARD)
    rate = jnp.where(fast, fast_rate, slow_rate)
    blocks = PACKED_TOKENS // TOKENS_PER_SHARD
    block_factor = jnp.exp(jax.random.uniform(parallel_lanes[2], (HEAD_COUNT, blocks, 1), jnp.float32, -jnp.log(2.0), jnp.log(2.0)))
    token_factor = jax.random.uniform(parallel_lanes[3], (HEAD_COUNT, blocks, TOKENS_PER_SHARD), jnp.float32, 0.5, 1.5)
    token_groups = jax.random.bernoulli(parallel_lanes[4], 2.0 / (LONGEST_DOC * TOKENS_PER_SHARD), (1, PACKED_TOKENS)).astype(jnp.float32)
    group_length = jax.random.uniform(parallel_lanes[5], (HEAD_COUNT, PACKED_TOKENS), jnp.float32, 0.223, 0.693)
    smoothed_values = (rate[:, None, None] * block_factor * token_factor).reshape(HEAD_COUNT, PACKED_TOKENS)
    return (smoothed_values + token_groups * group_length).astype(jnp.float32)


def draw_strengths(key, part):
    fast = head_speed(key)
    parallel_lanes = jax.random.split(jax.random.fold_in(key, 404), 3)
    slow_scale = jnp.exp(jax.random.uniform(parallel_lanes[0], (HEAD_COUNT,), jnp.float32, jnp.log(0.01), jnp.log(0.05)))
    fast_values = jax.random.uniform(parallel_lanes[1], (HEAD_COUNT, 2 * PACKED_TOKENS), jnp.float32, 0.3, 1.9)
    slow_values = slow_scale[:, None] * jax.random.uniform(parallel_lanes[2], (HEAD_COUNT, 2 * PACKED_TOKENS), jnp.float32, 0.5, 1.5)
    return jnp.where(fast[:, None], fast_values, slow_values).astype(jnp.float32)


def block_scale(key, shape, cuts, least, top_value):
    def one(axis_at, parts):
        heights = jax.random.uniform(jax.random.fold_in(jax.random.fold_in(key, 6), axis_at), (parts,), jnp.float32, least / len(cuts), top_value / len(cuts))
        return jnp.repeat(jnp.exp(heights), shape[axis_at] // parts).reshape((-1,) + (1,) * (len(shape) - axis_at - 1))

    loudness = one(*cuts[0])
    for cut in cuts[1:]:
        loudness = loudness * one(*cut)
    return loudness


def length_profile(count, total, reach, skew):
    portions = [(1 << 20) // math.isqrt(rank ** skew) + 1 for rank in range(2, count + 1)]
    spare, counts = total - reach - (count - 1), [1] * (count - 1)
    while spare > 0:
        candidates = [i for i in range(count - 1) if counts[i] < reach]
        whole, remaining = sum([portions[i] for i in candidates]), spare
        for i in candidates:
            extra = min(reach - counts[i], max(1, remaining * portions[i] // whole), spare)
            counts[i] = counts[i] + extra
            spare = spare - extra
    return np.array([reach] + counts)


def uneven(own_key, amount, total, bound, slope):
    if amount == 2:
        one = jax.random.randint(own_key, (), max(1, total - bound), min(bound, total - 1) + 1)
        return jnp.stack([one, total - one])
    tallies = jnp.asarray(length_profile(amount, total, bound, slope), jnp.int32)
    twos = (amount - 1) // 2
    source_of, sink = tallies[1:1 + 2 * twos:2], tallies[2:2 + 2 * twos:2]
    slack = jnp.minimum(source_of - 1, bound - sink)
    moved = jax.random.randint(jax.random.fold_in(own_key, 1), (twos,), 0, 1 << 20) % (slack + 1)
    tallies = tallies.at[1:1 + 2 * twos:2].set(source_of - moved).at[2:2 + 2 * twos:2].set(sink + moved)
    return tallies[jax.random.permutation(jax.random.fold_in(own_key, 2), amount)]


def normal_values(own_key, dims, deviation, reach, cuts=(), kind=jnp.bfloat16):
    gain = block_scale(own_key, dims, cuts, -0.22, 0.18) if cuts else 1.0
    result = jax.random.normal(own_key, dims, jnp.float32) * deviation * gain
    return jnp.minimum(jnp.maximum(result, -reach), reach).astype(kind)


def setup_inputs(seed: int = 0, part: int = 0) -> dict:
    arg_keys = jax.random.split(jax.random.key(seed), 10)
    own_keys = jax.random.split(jax.random.fold_in(arg_keys[9], part), 10)
    return {
        "queries": normal_values(own_keys[0], (HEAD_COUNT, PACKED_TOKENS, DK), 1.0, 6.0, ((1, 8),)),
        "key_pairs": normal_values(own_keys[1], (HEAD_COUNT, PACKED_TOKENS, 2 * DK), 1.0, 6.0, ((1, 8),)),
        "value_pairs": normal_values(own_keys[2], (HEAD_COUNT, PACKED_TOKENS, 2 * DV), 1.0, 6.0, ((1, 8),)),
        "strengths": draw_strengths(jax.random.fold_in(jax.random.fold_in(arg_keys[9], part), 71), part),
        "decays": draw_decays(jax.random.fold_in(jax.random.fold_in(arg_keys[9], part), 71), part),
        "conv_query": normal_values(arg_keys[5], (HEAD_COUNT, TAPS, DK), 0.5, 1.5, (), jnp.float32),
        "conv_key": normal_values(arg_keys[6], (HEAD_COUNT, TAPS, 2 * DK), 0.5, 1.5, (), jnp.float32),
        "conv_value": normal_values(arg_keys[7], (HEAD_COUNT, TAPS, 2 * DV), 0.5, 1.5, (), jnp.float32),
        "doc_lengths": uneven(own_keys[8], NDOCS, PACKED_TOKENS, MOST, 2).astype(jnp.int32),
    }


highest = lax.Precision.HIGHEST

def doc_starts(doc_lengths):
    ending = jnp.cumsum(doc_lengths).astype(jnp.int32)
    return (ending - doc_lengths).astype(jnp.int32)

def since_start(starts, offset, span_len):
    position = (offset + jnp.arange(span_len, dtype=jnp.int32)).astype(jnp.int32)
    reached = starts[None, :] <= position[:, None]
    latest = lax.optimization_barrier(jnp.max(jnp.where(reached, starts[None, :], 0), axis=1)).astype(jnp.int32)
    return (position - latest).astype(jnp.int32)

def short_conv(values, border, kernel, since):
    length = values.shape[1]
    border_len = border.shape[1]
    extended = jnp.concatenate([border, values], axis=1).astype(jnp.float32)
    summed = kernel[:, 0:1, :] * extended[:, border_len:, :]
    for lag_step in range(1, border_len + 1):
        shifted = extended[:, border_len - lag_step:border_len - lag_step + length, :]
        usable = (since >= lag_step)[None, :, None]
        summed = summed + jnp.where(usable, kernel[:, lag_step:lag_step + 1, :] * shifted, 0.0)
    return jax.nn.silu(summed)

def unit_rows(values, width):
    grouped = values.reshape(values.shape[0], -1, width)
    scale = lax.rsqrt(lax.optimization_barrier(jnp.sum(grouped * grouped, axis=-1, keepdims=True)) + 1e-06)
    return (grouped * scale).astype(jnp.bfloat16)

def prepare(queries, key_pairs, value_pairs, query_border, key_border, value_border, conv_query, conv_key, conv_value, since):
    heads = queries.shape[0]
    key_width = queries.shape[2]
    value_width = value_pairs.shape[2] // 2
    query_unit = unit_rows(short_conv(queries, query_border, conv_query, since), key_width)
    key_unit = unit_rows(short_conv(key_pairs, key_border, conv_key, since), key_width)
    value_unit = short_conv(value_pairs, value_border, conv_value, since).astype(jnp.bfloat16).reshape(heads, -1, value_width)
    return (query_unit, key_unit, value_unit)

def head_terms(query, keys, values, strength, decay, since):
    tokens_here = query.shape[0]
    steps = keys.shape[0]
    key_width = keys.shape[1]
    value_width = values.shape[1]
    log_gate = jnp.stack([-decay, jnp.zeros_like(decay)], axis=1).reshape(steps)
    opening = jnp.stack([since == 0, since < 0], axis=1).reshape(steps)
    running = jnp.cumsum(log_gate)
    segment = jnp.cumsum(opening.astype(jnp.int32)).astype(jnp.int32)
    sub_index = jnp.arange(steps, dtype=jnp.int32)
    linked = (segment[:, None] == segment[None, :]) & (sub_index[:, None] > sub_index[None, :])
    log_gap = jnp.where(linked, running[:, None] - running[None, :], 0.0)
    keys_wide = keys.astype(jnp.float32)
    intersection = jnp.einsum('sk,rk->sr', keys_wide, keys_wide, precision=highest)
    system = jnp.eye(steps, dtype=jnp.float32) + jnp.where(linked, strength[:, None] * jnp.exp(log_gap) * intersection, 0.0)
    open_gain = jnp.where(segment == 0, jnp.exp(running), 0.0)
    targets = jnp.concatenate([strength[:, None] * values.astype(jnp.float32), (strength * open_gain)[:, None] * keys_wide], axis=1)
    solved = jax.scipy.linalg.solve_triangular(system, targets, lower=True, unit_diagonal=True)
    end_gain = jnp.where(segment == segment[steps - 1], jnp.exp(running[steps - 1] - running), 0.0)
    weighted = keys_wide * end_gain[:, None]
    moved = jnp.einsum('nr,nk->rk', solved, weighted, precision=highest)
    transit = open_gain[steps - 1] * jnp.eye(key_width, dtype=jnp.float32) - moved[value_width:]
    carry_pair = jnp.concatenate([transit, moved[:value_width]], axis=0)
    out_rows = jnp.arange(tokens_here, dtype=jnp.int32) * 2 + 1
    out_segment = segment.reshape(tokens_here, 2)[:, 1]
    out_running = running.reshape(tokens_here, 2)[:, 1]
    reads = (out_segment[:, None] == segment[None, :]) & (out_rows[:, None] >= sub_index[None, :])
    read_gap = jnp.where(reads, out_running[:, None] - running[None, :], 0.0)
    query_wide = query.astype(jnp.float32)
    scores = jnp.einsum('ck,nk->cn', query_wide, keys_wide, precision=highest)
    mixing = jnp.where(reads, jnp.exp(read_gap) * scores, 0.0)
    gathered = jnp.dot(mixing.astype(jnp.float32), solved.astype(jnp.float32), precision=highest, preferred_element_type=jnp.float32)
    out_gain = open_gain.reshape(tokens_here, 2)[:, 1]
    correction = out_gain[:, None] * query_wide - gathered[:, value_width:]
    return (carry_pair, gathered[:, :value_width], correction)

def reference(queries, key_pairs, value_pairs, strengths, decays, conv_query, conv_key, conv_value, doc_lengths):
    starts = doc_starts(doc_lengths)
    heads = queries.shape[0]
    border_len = conv_query.shape[1] - 1

    def padded(values):
        return jnp.concatenate([jnp.zeros((heads, border_len, values.shape[2]), values.dtype), values], axis=1)
    padded_query = padded(queries)
    padded_key = padded(key_pairs)
    padded_value = padded(value_pairs)

    def one_stretch(state, index):
        offset = (index * TOKENS_PER_SHARD).astype(jnp.int32)
        since = since_start(starts, offset, TOKENS_PER_SHARD)

        def window(values):
            piece = lax.dynamic_slice_in_dim(values, offset, TOKENS_PER_SHARD + border_len, axis=1)
            return (piece[:, border_len:], piece[:, :border_len])
        query_here, query_border = window(padded_query)
        key_here, key_border = window(padded_key)
        value_here, value_border = window(padded_value)
        strength_here = lax.dynamic_slice_in_dim(strengths, (2 * offset).astype(jnp.int32), 2 * TOKENS_PER_SHARD, axis=1)
        decay_here = lax.dynamic_slice_in_dim(decays, offset, TOKENS_PER_SHARD, axis=1)
        query_unit, key_unit, value_unit = prepare(query_here, key_here, value_here, query_border, key_border, value_border, conv_query, conv_key, conv_value, since)

        def per_head(pieces):
            return head_terms(pieces[0], pieces[1], pieces[2], pieces[3], pieces[4], since)
        carry_pairs, local_out, correction = lax.map(per_head, (query_unit, key_unit, value_unit, strength_here, decay_here))
        stretch_out = (local_out + jnp.einsum('hck,hvk->hcv', correction, state, precision=highest)).astype(jnp.bfloat16)
        next_state = jnp.einsum('hvj,hjk->hvk', state, carry_pairs[:, :DK], precision=highest) + carry_pairs[:, DK:]
        return (next_state, stretch_out)
    initial = jnp.zeros((heads, DV, DK), jnp.float32)
    _, outputs = lax.scan(one_stretch, initial, jnp.arange(N_SEQ, dtype=jnp.int32))
    return jnp.transpose(outputs, (1, 0, 2, 3)).reshape(heads, PACKED_TOKENS, DV)
```

```python
import functools

import jax
import jax.numpy as jnp
from jax import lax
from jax.experimental import pallas as pl
from jax.experimental.pallas import tpu as pltpu
from jax.sharding import PartitionSpec as P

MESH = pl.DeviceIdType.MESH
BF = jnp.bfloat16
F32 = jnp.float32
FAR = -1e30
GROUP = 2
NT = (((1,), (1,)), ((), ()))


def mm(a, b):
    return jnp.dot(a.astype(BF), b.astype(BF), preferred_element_type=F32)


def split(a):
    high = a.astype(BF)
    return high, (a - high.astype(F32)).astype(BF)


def mm_wide(a, b):
    a_high, a_low = split(a)
    b_high, b_low = split(b)
    return mm(a_high, b_high) + (mm(a_high, b_low) + mm(a_low, b_high))


def exact_nt(a, b):
    return lax.dot_general(
        a, b, NT, precision=lax.Precision.HIGHEST, preferred_element_type=F32
    )


def iota(shape, axis):
    return lax.broadcasted_iota(jnp.int32, shape, axis)


def kernel(
    n_seq,
    docs_ref,
    q_ref,
    k_ref,
    v_ref,
    strength_ref,
    decay_ref,
    cq_ref,
    ck_ref,
    cv_ref,
    out_ref,
    bq_ref,
    bk_ref,
    bv_ref,
    ext_ref,
    usable_ref,
    bias_l_ref,
    bias_m_ref,
    open_col_ref,
    rows_ref,
    beta_cols_ref,
    run_cols_ref,
    run_rows_ref,
    maps_ref,
    terms_ref,
    arrived_ref,
    leaving_ref,
    border_send,
    border_recv,
    state_send,
    state_recv,
):
    heads, tokens, width = q_ref.shape
    half = tokens // 2
    steps = 2 * tokens
    pairs = heads // GROUP
    me = lax.axis_index("seq")
    offset = me * tokens
    has_left = me > 0
    has_right = me < n_seq - 1
    barrier = pltpu.get_barrier_semaphore()

    @pl.when(has_left)
    def _():
        pl.semaphore_signal(barrier, inc=1, device_id={"seq": me - 1}, device_id_type=MESH)

    def border_copies(pair):
        span = pl.ds(pair * GROUP, GROUP)
        return [
            pltpu.make_async_remote_copy(
                src_ref=source.at[span, pl.ds(tokens - 16, 16), :],
                dst_ref=target.at[span],
                send_sem=border_send.at[which, pair],
                recv_sem=border_recv.at[which, pair],
                device_id={"seq": me + 1},
                device_id_type=MESH,
            )
            for which, (source, target) in enumerate(
                [(q_ref, bq_ref), (k_ref, bk_ref), (v_ref, bv_ref)]
            )
        ]

    def state_copy(head):
        return pltpu.make_async_remote_copy(
            src_ref=leaving_ref.at[head],
            dst_ref=arrived_ref.at[head],
            send_sem=state_send.at[head],
            recv_sem=state_recv.at[head],
            device_id={"seq": me + 1},
            device_id_type=MESH,
        )

    @pl.when(has_right)
    def _():
        pl.semaphore_wait(barrier, 1)

        def send(pair, carry):
            for copy in border_copies(pair):
                copy.start()
            return carry

        lax.fori_loop(0, pairs, send, 0)

    @pl.when(me == 0)
    def _():
        bq_ref[...] = jnp.zeros_like(bq_ref)
        bk_ref[...] = jnp.zeros_like(bk_ref)
        bv_ref[...] = jnp.zeros_like(bv_ref)
        arrived_ref[...] = jnp.zeros_like(arrived_ref)

    def token_of(index):
        return (index // tokens) * half + index % half

    def sub_of(index):
        return 2 * token_of(index) + (index // half) % 2

    starts = []
    total = jnp.int32(0)
    for m in range(docs_ref.shape[0]):
        starts.append(total)
        total = total + docs_ref[m]

    def latest_of(position):
        latest = jnp.zeros_like(position)
        for start in starts:
            latest = jnp.maximum(latest, jnp.where(start <= position, start, 0))
        return latest

    token_col = token_of(iota((steps, tokens), 0))
    token_row = token_of(iota((8, steps), 1))
    latest_col = latest_of(offset + token_col)
    latest_row = latest_of(offset + token_row)
    position = offset + iota((tokens, tokens), 0)
    since = position - latest_of(position)
    for lag in range(1, 4):
        usable_ref[lag - 1] = jnp.where(since >= lag, 1.0, 0.0)
    sub_col = sub_of(iota((steps, steps), 0))
    sub_row = sub_of(iota((steps, steps), 1))
    wide_latest = jnp.concatenate([latest_col, latest_col], axis=1)
    same = wide_latest == latest_row[0:1]
    bias_l_ref[...] = jnp.where(same & (sub_col > sub_row), 0.0, FAR)
    reads = jnp.where(same & (sub_col + 1 >= sub_row), 0.0, FAR)
    bias_m_ref[...] = jnp.concatenate([reads[:half], reads[tokens : tokens + half]], axis=0)
    open_col_ref[...] = jnp.where(latest_col < offset, 0.0, FAR)
    last = token_row == tokens - 1
    final = jnp.max(latest_row, axis=1, keepdims=True)
    rows_ref[0] = jnp.where(latest_row == final, 0.0, FAR)
    rows_ref[1] = jnp.where(jnp.broadcast_to(final < offset, last.shape), 0.0, FAR)

    pick = jnp.where(sub_col == iota((steps, steps), 1), 1.0, 0.0)
    beta_cols_ref[...] = exact_nt(pick, strength_ref[...])
    summed = jnp.where(iota((steps, tokens), 1) <= token_col, -1.0, 0.0)
    run_cols_ref[...] = exact_nt(summed, decay_ref[...])
    run_rows_ref[...] = exact_nt(decay_ref[...], summed)

    lane_head = iota((steps, heads), 1)
    in_half = iota((tokens, tokens), 0) % half
    apart = in_half ^ (iota((tokens, tokens), 1) % half)
    eye = jnp.where(
        iota((tokens, tokens), 0) == iota((tokens, tokens), 1), 1.0, 0.0
    )
    eye_width = jnp.where(
        iota((width, width), 0) == iota((width, width), 1), 1.0, 0.0
    )
    both = range(GROUP)

    def convolved(u, head, lane, kernel_ref, column):
        here = slice(lane, lane + width)
        summed = kernel_ref[head, 0:1, column : column + width] * ext_ref[u, 16 : 16 + tokens, here]
        for lag in range(1, 4):
            shifted = ext_ref[u, 16 - lag : 16 - lag + tokens, here]
            tap = kernel_ref[head, lag : lag + 1, column : column + width]
            summed = summed + usable_ref[lag - 1] * (tap * shifted)
        return summed / (1.0 + jnp.exp(-summed))

    def unit(rows):
        scale = lax.rsqrt(jnp.sum(rows * rows, axis=1, keepdims=True) + 1e-6)
        return (rows * scale).astype(BF)

    def arranged(first, second):
        return jnp.concatenate([first[:half], second[:half], first[half:], second[half:]], axis=0)

    def one_j(rows):
        return jnp.concatenate([rows[:half], rows[tokens : tokens + half]], axis=0)

    def local(pair):
        ids = [pair * GROUP + u for u in both]
        for u in both:
            head = ids[u]
            ext_ref[u, 0:16, 0:width] = bq_ref[head].astype(F32)
            ext_ref[u, 0:16, width : 3 * width] = bk_ref[head].astype(F32)
            ext_ref[u, 0:16, 3 * width : 5 * width] = bv_ref[head].astype(F32)
            ext_ref[u, 16 : 16 + tokens, 0:width] = q_ref[head].astype(F32)
            ext_ref[u, 16 : 16 + tokens, width : 3 * width] = k_ref[head].astype(F32)
            ext_ref[u, 16 : 16 + tokens, 3 * width : 5 * width] = v_ref[head].astype(F32)
        query = [unit(convolved(u, ids[u], 0, cq_ref, 0)) for u in both]
        keys = [
            arranged(
                unit(convolved(u, ids[u], width, ck_ref, 0)),
                unit(convolved(u, ids[u], 2 * width, ck_ref, width)),
            )
            for u in both
        ]
        values = [
            arranged(
                convolved(u, ids[u], 3 * width, cv_ref, 0).astype(BF),
                convolved(u, ids[u], 4 * width, cv_ref, width).astype(BF),
            )
            for u in both
        ]
        beta = [
            jnp.sum(jnp.where(lane_head == ids[u], beta_cols_ref[...], 0.0), axis=1, keepdims=True)
            for u in both
        ]
        run_col = [
            jnp.sum(jnp.where(lane_head == ids[u], run_cols_ref[...], 0.0), axis=1, keepdims=True)
            for u in both
        ]
        run_row = [run_rows_ref[pl.ds(ids[u], 1), :] for u in both]
        run_last = [
            jnp.sum(
                jnp.where(iota((1, steps), 1) == steps - 1, run_row[u], 0.0), axis=1, keepdims=True
            )
            for u in both
        ]
        products = [
            lax.dot_general(
                jnp.concatenate([keys[u], query[u], eye_width.astype(BF)], axis=0),
                keys[u],
                NT,
                preferred_element_type=F32,
            )
            for u in both
        ]
        system = []
        for u in both:
            top = jnp.exp(run_col[u][:tokens] - run_row[u][:, :tokens] + bias_l_ref[:tokens, :tokens])
            low = jnp.exp(run_col[u][tokens:] - run_row[u] + bias_l_ref[tokens:, :])
            top = top * (beta[u][:tokens] * products[u][:tokens, :tokens])
            low = low * (beta[u][tokens:] * products[u][tokens:steps])
            system.append((top, low[:, :tokens].astype(BF), low[:, tokens:]))
        blocks = [system[u][side] for u in both for side in (0, 2)]
        inverse = [eye - jnp.where(apart == 0, block, 0.0) for block in blocks]
        level = 1
        while level < half:
            at_level = (apart >= level) & (apart < 2 * level)
            narrow = [x.astype(BF) for x in inverse]
            inner = [
                mm(jnp.where(at_level, block, 0.0), x) for block, x in zip(blocks, narrow)
            ]
            inverse = [x - mm(n, y) for x, n, y in zip(inverse, narrow, inner)]
            level *= 2
        inverse = [x.astype(BF) for x in inverse]
        opened = [jnp.exp(run_col[u] + open_col_ref[...]) for u in both]
        targets = [
            jnp.concatenate(
                [
                    beta[u] * values[u].astype(F32),
                    (beta[u] * opened[u]) * keys[u].astype(F32),
                ],
                axis=1,
            )
            for u in both
        ]
        first = [mm(inverse[2 * u], targets[u][:tokens]) for u in both]
        second = [targets[u][tokens:] - mm(system[u][1], first[u]) for u in both]
        second = [mm(inverse[2 * u + 1], second[u]) for u in both]
        solved = [jnp.concatenate([first[u], second[u]], axis=0) for u in both]
        readers = []
        for u in both:
            mixing = jnp.exp(one_j(run_col[u]) - run_row[u] + bias_m_ref[...])
            mixing = mixing * products[u][steps : steps + tokens]
            to_end = jnp.exp(run_last[u] - run_row[u] + rows_ref[0, 0:1, :])
            readers.append(
                jnp.concatenate([to_end * products[u][steps + tokens :], mixing], axis=0)
            )
        gathered = [mm_wide(readers[u], solved[u]) for u in both]
        for u in both:
            through = jnp.exp(run_last[u] + rows_ref[1, 0:1, :width])
            transit = through * eye_width - gathered[u][:width, width:]
            correction = one_j(opened[u]) * query[u].astype(F32) - gathered[u][width:, width:]
            maps_ref[ids[u]] = jnp.concatenate([transit, correction], axis=0).astype(BF)
            terms_ref[ids[u]] = gathered[u][:, :width]

    def chain(pair):
        for u in both:
            head = pair * GROUP + u

            @pl.when(has_left)
            def _():
                state_copy(head).wait_recv()

            result = terms_ref[head] + mm(maps_ref[head], arrived_ref[head])

            @pl.when(has_right)
            def _():
                leaving_ref[head] = result[:width].astype(BF)
                state_copy(head).start()

            out_ref[head] = result[width:].astype(BF)

    def turn(step, carry):
        @pl.when(step < pairs)
        def _():
            @pl.when(has_left)
            def _():
                for copy in border_copies(step):
                    copy.wait_recv()

            local(step)

        ready = step - me

        @pl.when((ready >= 0) & (ready < pairs))
        def _():
            chain(ready)

        return carry

    lax.fori_loop(0, pairs + n_seq - 1, turn, 0)

    @pl.when(has_right)
    def _():
        def finish(pair, carry):
            for copy in border_copies(pair):
                copy.wait_send()
            for u in both:
                state_copy(pair * GROUP + u).wait_send()
            return carry

        lax.fori_loop(0, pairs, finish, 0)


def body(
    queries,
    key_pairs,
    value_pairs,
    strengths,
    decays,
    conv_query,
    conv_key,
    conv_value,
    doc_lengths,
):
    heads, tokens, width = queries.shape
    n_seq = lax.axis_size("seq")
    steps = 2 * tokens
    pairs = heads // GROUP
    vmem = pl.BlockSpec(memory_space=pltpu.VMEM)
    return pl.pallas_call(
        functools.partial(kernel, n_seq),
        out_shape=jax.ShapeDtypeStruct((heads, tokens, width), BF),
        in_specs=[pl.BlockSpec(memory_space=pltpu.SMEM)] + [vmem] * 8,
        out_specs=vmem,
        scratch_shapes=[
            pltpu.VMEM((heads, 16, width), BF),
            pltpu.VMEM((heads, 16, 2 * width), BF),
            pltpu.VMEM((heads, 16, 2 * width), BF),
            pltpu.VMEM((GROUP, 16 + tokens, 5 * width), F32),
            pltpu.VMEM((3, tokens, tokens), F32),
            pltpu.VMEM((steps, steps), F32),
            pltpu.VMEM((tokens, steps), F32),
            pltpu.VMEM((steps, tokens), F32),
            pltpu.VMEM((2, 8, steps), F32),
            pltpu.VMEM((steps, heads), F32),
            pltpu.VMEM((steps, heads), F32),
            pltpu.VMEM((heads, steps), F32),
            pltpu.VMEM((heads, 2 * width, width), BF),
            pltpu.VMEM((heads, 2 * width, width), F32),
            pltpu.VMEM((heads, width, width), BF),
            pltpu.VMEM((heads, width, width), BF),
            pltpu.SemaphoreType.DMA((3, pairs)),
            pltpu.SemaphoreType.DMA((3, pairs)),
            pltpu.SemaphoreType.DMA((heads,)),
            pltpu.SemaphoreType.DMA((heads,)),
        ],
        compiler_params=pltpu.CompilerParams(
            collective_id=0, has_side_effects=True, vmem_limit_bytes=48 << 20
        ),
        name="delta_product",
    )(
        doc_lengths,
        queries,
        key_pairs,
        value_pairs,
        strengths,
        decays,
        conv_query,
        conv_key,
        conv_value,
    )


def solution(mesh):
    in_specs = (
        P(None, ("dp", "seq"), None),
        P(None, ("dp", "seq"), None),
        P(None, ("dp", "seq"), None),
        P(None, ("dp", "seq")),
        P(None, ("dp", "seq")),
        P(),
        P(),
        P(),
        P("dp"),
    )
    out_specs = P(None, ("dp", "seq"), None)
    return jax.shard_map(body, mesh=mesh, in_specs=in_specs, out_specs=out_specs, check_vma=False)
```

```python
import functools

import jax
import jax.numpy as jnp
from jax import lax
from jax.experimental import pallas as pl
from jax.experimental.pallas import tpu as pltpu
from jax.sharding import PartitionSpec as P

MESH = pl.DeviceIdType.MESH
BF = jnp.bfloat16
F32 = jnp.float32
FAR = -1e30
GROUP = 8
PART = 4
NT = (((1,), (1,)), ((), ()))


def mm(a, b):
    return jnp.dot(a.astype(BF), b.astype(BF), preferred_element_type=F32)


def split(a):
    high = a.astype(BF)
    return high, (a - high.astype(F32)).astype(BF)


def mm_wide(a, b):
    a_high, a_low = split(a)
    b_high, b_low = split(b)
    return mm(a_high, b_high) + (mm(a_high, b_low) + mm(a_low, b_high))


def exact_nt(a, b):
    return lax.dot_general(
        a, b, NT, precision=lax.Precision.HIGHEST, preferred_element_type=F32
    )


def iota(shape, axis):
    return lax.broadcasted_iota(jnp.int32, shape, axis)


def kernel(
    n_seq,
    docs_hbm,
    q_hbm,
    k_hbm,
    v_hbm,
    strength_hbm,
    decay_hbm,
    cq_hbm,
    ck_hbm,
    cv_hbm,
    out_ref,
    docs_ref,
    q_ref,
    k_ref,
    v_ref,
    strength_ref,
    decay_ref,
    cq_ref,
    ck_ref,
    cv_ref,
    bq_ref,
    bk_ref,
    bv_ref,
    ext_ref,
    usable_ref,
    bias_l_ref,
    bias_m_ref,
    open_col_ref,
    rows_ref,
    beta_cols_ref,
    run_cols_ref,
    run_rows_ref,
    keys_ref,
    solved_ref,
    terms_ref,
    transit_ref,
    local_ref,
    correction_ref,
    arrived_ref,
    leaving_ref,
    pair_in_ref,
    pair_out_ref,
    load_sem,
    border_send,
    border_recv,
    pair_send,
    pair_recv,
    state_send,
    state_recv,
    back_send,
    back_recv,
):
    heads, tokens, width = q_ref.shape
    half = tokens // 2
    steps = 2 * tokens
    parts = heads // PART
    me = lax.axis_index("seq")
    chip = me // 2
    chips = n_seq // 2
    upper = me % 2 == 1
    lower = me % 2 == 0
    offset = me * tokens
    has_left = me > 0
    has_right = me < n_seq - 1
    passes_on = upper & has_right
    barrier = pltpu.get_barrier_semaphore()

    @pl.when(has_left)
    def _():
        pl.semaphore_signal(barrier, inc=1, device_id={"seq": me - 1}, device_id_type=MESH)

    @pl.when(upper & (chip > 0))
    def _():
        pl.semaphore_signal(barrier, inc=1, device_id={"seq": me - 2}, device_id_type=MESH)

    @pl.when(lower)
    def _():
        pl.semaphore_signal(barrier, inc=1, device_id={"seq": me + 1}, device_id_type=MESH)

    spans = [pl.ds(0, GROUP), pl.ds(GROUP, heads - GROUP)]
    wide = [(q_hbm, q_ref), (k_hbm, k_ref), (v_hbm, v_ref)]
    small = [
        (docs_hbm, docs_ref),
        (decay_hbm, decay_ref),
        (strength_hbm, strength_ref),
        (cq_hbm, cq_ref),
        (ck_hbm, ck_ref),
        (cv_hbm, cv_ref),
    ]
    small_loads = [
        pltpu.make_async_copy(source, target, load_sem.at[i])
        for i, (source, target) in enumerate(small)
    ]
    wide_loads = [
        [
            pltpu.make_async_copy(
                source.at[span], target.at[span], load_sem.at[len(small) + 3 * part + i]
            )
            for i, (source, target) in enumerate(wide)
        ]
        for part, span in enumerate(spans)
    ]
    for copy in small_loads + wide_loads[0] + wide_loads[1]:
        copy.start()

    def border_copies(part):
        return [
            pltpu.make_async_remote_copy(
                src_ref=source.at[spans[part], pl.ds(tokens - 16, 16), :],
                dst_ref=target.at[spans[part]],
                send_sem=border_send.at[which, part],
                recv_sem=border_recv.at[which, part],
                device_id={"seq": me + 1},
                device_id_type=MESH,
            )
            for which, (source, target) in enumerate(
                [(q_hbm, bq_ref), (k_hbm, bk_ref), (v_hbm, bv_ref)]
            )
        ]

    def pair_copy(head):
        return pltpu.make_async_remote_copy(
            src_ref=pair_out_ref.at[head],
            dst_ref=pair_in_ref.at[head],
            send_sem=pair_send.at[head],
            recv_sem=pair_recv.at[head],
            device_id={"seq": me + 1},
            device_id_type=MESH,
        )

    def state_copy(head):
        return pltpu.make_async_remote_copy(
            src_ref=leaving_ref.at[head],
            dst_ref=arrived_ref.at[head],
            send_sem=state_send.at[head],
            recv_sem=state_recv.at[head],
            device_id={"seq": me + 2},
            device_id_type=MESH,
        )

    def back_copy(head):
        return pltpu.make_async_remote_copy(
            src_ref=arrived_ref.at[head],
            dst_ref=arrived_ref.at[head],
            send_sem=back_send.at[head],
            recv_sem=back_recv.at[head],
            device_id={"seq": me - 1},
            device_id_type=MESH,
        )

    def send_borders():
        for part in range(2):
            for copy in border_copies(part):
                copy.start()

    @pl.when(lower)
    def _():
        pl.semaphore_wait(barrier, 1)
        send_borders()

    @pl.when(passes_on)
    def _():
        pl.semaphore_wait(barrier, 3)
        send_borders()

    @pl.when(me == n_seq - 1)
    def _():
        pl.semaphore_wait(barrier, 1)

    @pl.when(me == 0)
    def _():
        bq_ref[...] = jnp.zeros_like(bq_ref)
        bk_ref[...] = jnp.zeros_like(bk_ref)
        bv_ref[...] = jnp.zeros_like(bv_ref)

    @pl.when(chip == 0)
    def _():
        arrived_ref[...] = jnp.zeros_like(arrived_ref)

    for copy in small_loads:
        copy.wait()

    def token_of(index):
        return (index // tokens) * half + index % half

    def sub_of(index):
        return 2 * token_of(index) + (index // half) % 2

    starts = []
    total = jnp.int32(0)
    for m in range(docs_ref.shape[0]):
        starts.append(total)
        total = total + docs_ref[m]

    def latest_of(position):
        latest = jnp.zeros_like(position)
        for start in starts:
            latest = jnp.maximum(latest, jnp.where(start <= position, start, 0))
        return latest

    token_col = token_of(iota((steps, tokens), 0))
    token_row = token_of(iota((8, steps), 1))
    latest_col = latest_of(offset + token_col)
    latest_row = latest_of(offset + token_row)
    position = offset + iota((tokens, tokens), 0)
    since = position - latest_of(position)
    for lag in range(1, 4):
        usable_ref[lag - 1] = jnp.where(since >= lag, 1.0, 0.0)
    sub_col = sub_of(iota((steps, steps), 0))
    sub_row = sub_of(iota((steps, steps), 1))
    wide_latest = jnp.concatenate([latest_col, latest_col], axis=1)
    same = wide_latest == latest_row[0:1]
    bias_l_ref[...] = jnp.where(same & (sub_col > sub_row), 0.0, FAR)
    reads = jnp.where(same & (sub_col + 1 >= sub_row), 0.0, FAR)
    bias_m_ref[...] = jnp.concatenate([reads[:half], reads[tokens : tokens + half]], axis=0)
    open_col_ref[...] = jnp.where(latest_col < offset, 0.0, FAR)
    last = token_row == tokens - 1
    final = jnp.max(latest_row, axis=1, keepdims=True)
    rows_ref[0] = jnp.where(latest_row == final, 0.0, FAR)
    rows_ref[1] = jnp.where(jnp.broadcast_to(final < offset, last.shape), 0.0, FAR)

    pick = jnp.where(sub_col == iota((steps, steps), 1), 1.0, 0.0)
    beta_cols_ref[...] = exact_nt(pick, strength_ref[...])
    summed = jnp.where(iota((steps, tokens), 1) <= token_col, -1.0, 0.0)
    run_cols_ref[...] = exact_nt(summed, decay_ref[...])
    run_rows_ref[...] = exact_nt(decay_ref[...], summed)

    lane_head = iota((steps, heads), 1)
    in_half = iota((tokens, tokens), 0) % half
    apart = in_half ^ (iota((tokens, tokens), 1) % half)
    eye = jnp.where(
        iota((tokens, tokens), 0) == iota((tokens, tokens), 1), 1.0, 0.0
    )
    eye_width = jnp.where(
        iota((width, width), 0) == iota((width, width), 1), 1.0, 0.0
    )
    both = range(GROUP)

    def convolved(u, head, lane, kernel_ref, column):
        here = slice(lane, lane + width)
        summed = kernel_ref[head, 0:1, column : column + width] * ext_ref[u, 16 : 16 + tokens, here]
        for lag in range(1, 4):
            shifted = ext_ref[u, 16 - lag : 16 - lag + tokens, here]
            tap = kernel_ref[head, lag : lag + 1, column : column + width]
            summed = summed + usable_ref[lag - 1] * (tap * shifted)
        return summed / (1.0 + jnp.exp(-summed))

    def unit(rows):
        scale = lax.rsqrt(jnp.sum(rows * rows, axis=1, keepdims=True) + 1e-6)
        return (rows * scale).astype(BF)

    def arranged(first, second):
        return jnp.concatenate([first[:half], second[:half], first[half:], second[half:]], axis=0)

    def one_j(rows):
        return jnp.concatenate([rows[:half], rows[tokens : tokens + half]], axis=0)

    def local(pair):
        ids = [pair * GROUP + u for u in both]
        for u in both:
            head = ids[u]
            ext_ref[u, 0:16, width : 3 * width] = bk_ref[head].astype(F32)
            ext_ref[u, 0:16, 3 * width : 5 * width] = bv_ref[head].astype(F32)
            ext_ref[u, 16 : 16 + tokens, width : 3 * width] = k_ref[head].astype(F32)
            ext_ref[u, 16 : 16 + tokens, 3 * width : 5 * width] = v_ref[head].astype(F32)
        keys = [
            arranged(
                unit(convolved(u, ids[u], width, ck_ref, 0)),
                unit(convolved(u, ids[u], 2 * width, ck_ref, width)),
            )
            for u in both
        ]
        values = [
            arranged(
                convolved(u, ids[u], 3 * width, cv_ref, 0).astype(BF),
                convolved(u, ids[u], 4 * width, cv_ref, width).astype(BF),
            )
            for u in both
        ]
        beta = [
            jnp.sum(jnp.where(lane_head == ids[u], beta_cols_ref[...], 0.0), axis=1, keepdims=True)
            for u in both
        ]
        run_col = [
            jnp.sum(jnp.where(lane_head == ids[u], run_cols_ref[...], 0.0), axis=1, keepdims=True)
            for u in both
        ]
        run_row = [run_rows_ref[pl.ds(ids[u], 1), :] for u in both]
        run_last = [
            jnp.sum(
                jnp.where(iota((1, steps), 1) == steps - 1, run_row[u], 0.0), axis=1, keepdims=True
            )
            for u in both
        ]
        products = [
            lax.dot_general(
                jnp.concatenate([keys[u], eye_width.astype(BF)], axis=0),
                keys[u],
                NT,
                preferred_element_type=F32,
            )
            for u in both
        ]
        system = []
        for u in both:
            top = jnp.exp(run_col[u][:tokens] - run_row[u][:, :tokens] + bias_l_ref[:tokens, :tokens])
            low = jnp.exp(run_col[u][tokens:] - run_row[u] + bias_l_ref[tokens:, :])
            top = top * (beta[u][:tokens] * products[u][:tokens, :tokens])
            low = low * (beta[u][tokens:] * products[u][tokens:steps])
            system.append((top, low[:, :tokens].astype(BF), low[:, tokens:]))
        blocks = [system[u][side] for u in both for side in (0, 2)]
        inverse = [eye - jnp.where(apart == 0, block, 0.0) for block in blocks]
        level = 1
        while level < half:
            at_level = (apart >= level) & (apart < 2 * level)
            narrow = [x.astype(BF) for x in inverse]
            inner = [
                mm(jnp.where(at_level, block, 0.0), x) for block, x in zip(blocks, narrow)
            ]
            inverse = [x - mm(n, y) for x, n, y in zip(inverse, narrow, inner)]
            level *= 2
        inverse = [x.astype(BF) for x in inverse]
        opened = [jnp.exp(run_col[u] + open_col_ref[...]) for u in both]
        targets = [
            jnp.concatenate(
                [
                    beta[u] * values[u].astype(F32),
                    (beta[u] * opened[u]) * keys[u].astype(F32),
                ],
                axis=1,
            )
            for u in both
        ]
        first = [mm(inverse[2 * u], targets[u][:tokens]) for u in both]
        second = [targets[u][tokens:] - mm(system[u][1], first[u]) for u in both]
        second = [mm(inverse[2 * u + 1], second[u]) for u in both]
        solved = [jnp.concatenate([first[u], second[u]], axis=0) for u in both]
        to_end = [
            (jnp.exp(run_last[u] - run_row[u] + rows_ref[0, 0:1, :]) * products[u][steps:]).astype(BF)
            for u in both
        ]
        moved = [mm(to_end[u], solved[u]) for u in both]
        for u in both:
            through = jnp.exp(run_last[u] + rows_ref[1, 0:1, :width])
            transit = (through * eye_width - moved[u][:, width:]).astype(BF)
            terms_ref[ids[u]] = moved[u][:, :width]
            transit_ref[ids[u]] = transit
            pair_out_ref[ids[u]] = jnp.concatenate([moved[u][:, :width].astype(BF), transit], axis=1)
            keys_ref[ids[u]] = keys[u]
            solved_ref[ids[u]] = solved[u]

    some = range(PART)

    def read_local(part):
        ids = [part * PART + u for u in some]
        for u in some:
            ext_ref[u, 0:16, 0:width] = bq_ref[ids[u]].astype(F32)
            ext_ref[u, 16 : 16 + tokens, 0:width] = q_ref[ids[u]].astype(F32)
        query = [unit(convolved(u, ids[u], 0, cq_ref, 0)) for u in some]
        run_col = [
            jnp.sum(
                jnp.where(lane_head[:tokens] == ids[u], one_j(run_cols_ref[...]), 0.0),
                axis=1,
                keepdims=True,
            )
            for u in some
        ]
        scores = [
            lax.dot_general(query[u], keys_ref[ids[u]], NT, preferred_element_type=F32)
            for u in some
        ]
        mixing = [
            jnp.exp(run_col[u] - run_rows_ref[pl.ds(ids[u], 1), :] + bias_m_ref[...]) * scores[u]
            for u in some
        ]
        gathered = [mm_wide(mixing[u], solved_ref[ids[u]]) for u in some]
        for u in some:
            opened = jnp.exp(run_col[u] + one_j(open_col_ref[...]))
            correction = opened * query[u].astype(F32) - gathered[u][:, width:]
            correction_ref[ids[u]] = correction.astype(BF)
            local_ref[ids[u]] = gathered[u][:, :width]

    def compose(part):
        ids = [part * PART + u for u in some]
        for head in ids:
            pair_copy(head).wait_recv()
        composed = [mm(transit_ref[head], pair_in_ref[head]) for head in ids]
        for head, both_maps in zip(ids, composed):
            terms_ref[head] = terms_ref[head] + both_maps[:, :width]
            transit_ref[head] = both_maps[:, width:].astype(BF)

    def chain(part):
        ids = [part * PART + u for u in some]

        @pl.when(chip > 0)
        def _():
            for head in ids:
                state_copy(head).wait_recv()

        @pl.when(has_right)
        def _():
            ends = [terms_ref[head] + mm(transit_ref[head], arrived_ref[head]) for head in ids]
            for head, end in zip(ids, ends):
                leaving_ref[head] = end.astype(BF)
            for head in ids:
                state_copy(head).start()

        @pl.when(chip > 0)
        def _():
            for head in ids:
                back_copy(head).start()

    def read_upper(part):
        ids = [part * PART + u for u in some]
        inner = [
            mm(pair_in_ref[head, :, width:], arrived_ref[head])
            + pair_in_ref[head, :, :width].astype(F32)
            for head in ids
        ]
        reads = [
            local_ref[head] + mm(correction_ref[head], state) for head, state in zip(ids, inner)
        ]
        for head, rows in zip(ids, reads):
            out_ref[head] = rows.astype(BF)

    def read_lower(part):
        ids = [part * PART + u for u in some]

        @pl.when(chip > 0)
        def _():
            for head in ids:
                back_copy(head).wait_recv()

        reads = [local_ref[head] + mm(correction_ref[head], arrived_ref[head]) for head in ids]
        for head, rows in zip(ids, reads):
            out_ref[head] = rows.astype(BF)

    def first_phase(step, carry):
        for part in range(2):

            @pl.when(step == part)
            def _():
                for copy in wide_loads[part]:
                    copy.wait()

                @pl.when(has_left)
                def _():
                    for copy in border_copies(part):
                        copy.wait_recv()

        local(step)

        @pl.when(lower)
        def _():
            for u in both:
                pair_copy(step * GROUP + u).start()

        return carry

    lax.fori_loop(0, heads // GROUP, first_phase, 0)

    def second_phase(step, carry):
        ready = step - chip

        @pl.when(upper & (step < parts))
        def _():
            compose(step)

        @pl.when(upper & (ready >= 0) & (ready < parts))
        def _():
            chain(ready)

        @pl.when(step < parts)
        def _():
            read_local(step)

        @pl.when(upper & (ready >= 0) & (ready < parts))
        def _():
            read_upper(ready)

        @pl.when(lower & (ready >= 1) & (ready <= parts))
        def _():
            read_lower(ready - 1)

        return carry

    lax.fori_loop(0, parts + chips, second_phase, 0)

    @pl.when(has_right)
    def _():
        for part in range(2):
            for copy in border_copies(part):
                copy.wait_send()

    @pl.when(lower)
    def _():
        def finish(head, carry):
            pair_copy(head).wait_send()
            return carry

        lax.fori_loop(0, heads, finish, 0)

    @pl.when(passes_on)
    def _():
        def finish(head, carry):
            state_copy(head).wait_send()
            return carry

        lax.fori_loop(0, heads, finish, 0)

    @pl.when(upper & (chip > 0))
    def _():
        def finish(head, carry):
            back_copy(head).wait_send()
            return carry

        lax.fori_loop(0, heads, finish, 0)


def body(
    queries,
    key_pairs,
    value_pairs,
    strengths,
    decays,
    conv_query,
    conv_key,
    conv_value,
    doc_lengths,
):
    heads, tokens, width = queries.shape
    n_seq = lax.axis_size("seq")
    steps = 2 * tokens
    vmem = pl.BlockSpec(memory_space=pltpu.VMEM)
    return pl.pallas_call(
        functools.partial(kernel, n_seq),
        out_shape=jax.ShapeDtypeStruct((heads, tokens, width), BF),
        in_specs=[pl.BlockSpec(memory_space=pltpu.HBM)] * 9,
        out_specs=vmem,
        scratch_shapes=[
            pltpu.SMEM(doc_lengths.shape, jnp.int32),
            pltpu.VMEM(queries.shape, BF),
            pltpu.VMEM(key_pairs.shape, BF),
            pltpu.VMEM(value_pairs.shape, BF),
            pltpu.VMEM(strengths.shape, F32),
            pltpu.VMEM(decays.shape, F32),
            pltpu.VMEM(conv_query.shape, F32),
            pltpu.VMEM(conv_key.shape, F32),
            pltpu.VMEM(conv_value.shape, F32),
            pltpu.VMEM((heads, 16, width), BF),
            pltpu.VMEM((heads, 16, 2 * width), BF),
            pltpu.VMEM((heads, 16, 2 * width), BF),
            pltpu.VMEM((GROUP, 16 + tokens, 5 * width), F32),
            pltpu.VMEM((3, tokens, tokens), F32),
            pltpu.VMEM((steps, steps), F32),
            pltpu.VMEM((tokens, steps), F32),
            pltpu.VMEM((steps, tokens), F32),
            pltpu.VMEM((2, 8, steps), F32),
            pltpu.VMEM((steps, heads), F32),
            pltpu.VMEM((steps, heads), F32),
            pltpu.VMEM((heads, steps), F32),
            pltpu.VMEM((heads, steps, width), BF),
            pltpu.VMEM((heads, steps, 2 * width), F32),
            pltpu.VMEM((heads, width, width), F32),
            pltpu.VMEM((heads, width, width), BF),
            pltpu.VMEM((heads, tokens, width), F32),
            pltpu.VMEM((heads, tokens, width), BF),
            pltpu.VMEM((heads, width, width), BF),
            pltpu.VMEM((heads, width, width), BF),
            pltpu.VMEM((heads, width, 2 * width), BF),
            pltpu.VMEM((heads, width, 2 * width), BF),
            pltpu.SemaphoreType.DMA((12,)),
            pltpu.SemaphoreType.DMA((3, 2)),
            pltpu.SemaphoreType.DMA((3, 2)),
            pltpu.SemaphoreType.DMA((heads,)),
            pltpu.SemaphoreType.DMA((heads,)),
            pltpu.SemaphoreType.DMA((heads,)),
            pltpu.SemaphoreType.DMA((heads,)),
            pltpu.SemaphoreType.DMA((heads,)),
            pltpu.SemaphoreType.DMA((heads,)),
        ],
        compiler_params=pltpu.CompilerParams(
            collective_id=0, has_side_effects=True, vmem_limit_bytes=60 << 20
        ),
        name="delta_product",
    )(
        doc_lengths,
        queries,
        key_pairs,
        value_pairs,
        strengths,
        decays,
        conv_query,
        conv_key,
        conv_value,
    )


def solution(mesh):
    in_specs = (
        P(None, ("dp", "seq"), None),
        P(None, ("dp", "seq"), None),
        P(None, ("dp", "seq"), None),
        P(None, ("dp", "seq")),
        P(None, ("dp", "seq")),
        P(),
        P(),
        P(),
        P("dp"),
    )
    out_specs = P(None, ("dp", "seq"), None)
    return jax.shard_map(body, mesh=mesh, in_specs=in_specs, out_specs=out_specs, check_vma=False)
```
